32 devices in a mesh: slab: 4 (over y, x), cross: 8 (over z, core).
Axes of the slice: x: 2, y: 2, z: 4, core: 2. Of those that a mesh axis runs over, the one named last changes fastest.
Arguments:
- rhs: bfloat16 [4, 8, 32, 128, 128], P('slab', 'cross'), may hold values from -6 to 6
- m_blocks: bfloat16 [4, 8, 56, 3, 128, 128], P('slab', 'cross'), may hold values from -0.3125 to 0.3125
- m_cols: int32 [4, 8, 56, 3], P('slab', 'cross'), may hold values from 0 to 55, as said below
- j_blocks: bfloat16 [4, 8, 32, 3, 128, 128], P('slab', 'cross'), may hold values from -0.3125 to 0.3125
- j_cols: int32 [4, 8, 32, 3], P('slab', 'cross'), may hold values from 0 to 55, as said below
- send_list: int32 [4, 8, 8, 2], P('slab', 'cross'), may hold values from 0 to 31, as said below
- send_count: int32 [4, 8, 8], P('slab', 'cross'), may hold values from 0 to 2, as said below
Outputs:
- second_iterate: bfloat16 [4, 8, 32, 128, 128], P('slab', 'cross')
The draws below stay inside these ranges and needn't reach their ends.
Inputs may be any that keep to these rules, and one draw needn't show every extreme that they name: `m_cols`: each row's first block column is the row itself; the others differ from it and from each other. `j_cols`: each row's first block column is the row itself; the others differ from it and from each other. `send_list`: the used slots of one list name different block rows. `send_count`: no subdomain lends rows to itself; in every slab index some subdomain receives 2 rows from each other one.
All inputs are finite; a program needn't handle non-finite values.
Results may differ from the reference program's by a relative error of at most 0.0058.
Values may be sent and summed in bfloat16 or wider, within the bound.
A program may use at most 64 MiB of HBM per device.

```python
import jax
import jax.numpy as jnp
from jax import lax

BLK = 128
NV = 128
ROWS = 32
OVL = 4
CAP = 2
NBLK = 3
EXT = 56
N_SLAB = 4
N_CROSS = 8


def pattern_cols(key, row_total, span):
    leading = (N_SLAB, N_CROSS, row_total)
    row_ids = jnp.arange(row_total, dtype=jnp.int32)
    columns = [jnp.broadcast_to(row_ids, leading)]
    for slot_num in range(1, NBLK):
        lower_end = 1 + (slot_num - 1) * (span - 1) // (NBLK - 1)
        upper_end = 1 + slot_num * (span - 1) // (NBLK - 1)
        offset = jax.random.randint(jax.random.fold_in(key, slot_num), leading, lower_end, upper_end, dtype=jnp.int32)
        columns.append((row_ids + offset) % span)
    return jnp.stack(columns, axis=-1)


def draw_m_cols(key, part):
    return pattern_cols(jax.random.fold_in(key, 11), EXT, EXT)


def draw_j_cols(key, part):
    columns = pattern_cols(jax.random.fold_in(key, 23), ROWS, EXT)
    return columns.at[0, 0, 0, NBLK - 1].set(EXT - 1)


def draw_send_count(key, part):
    counts = jax.random.randint(jax.random.fold_in(key, 31), (N_SLAB, N_CROSS, N_CROSS), 0, CAP + 1, dtype=jnp.int32)
    chosen = jax.random.randint(jax.random.fold_in(key, 37), (N_SLAB,), 0, N_CROSS, dtype=jnp.int32)
    peer_ids = jnp.arange(N_CROSS, dtype=jnp.int32)
    filled = peer_ids[None, None, :] == chosen[:, None, None]
    counts = jnp.where(filled, CAP, counts)
    itself = peer_ids[None, :, None] == peer_ids[None, None, :]
    return jnp.where(itself, 0, counts).astype(jnp.int32)


def draw_send_list(key, part):
    starts = jax.random.randint(jax.random.fold_in(key, 41), (N_SLAB, N_CROSS, N_CROSS), 0, ROWS, dtype=jnp.int32)
    starts = starts.at[0, 0, 0].set(ROWS - 1).at[0, 0, 1].set(0)
    slots = [starts]
    for slot_num in range(1, CAP):
        lower_end = slot_num * ROWS // CAP
        upper_end = (slot_num + 1) * ROWS // CAP
        offset = jax.random.randint(jax.random.fold_in(key, 50 + slot_num), (N_SLAB, N_CROSS, N_CROSS), lower_end, upper_end, dtype=jnp.int32)
        slots.append((starts + offset) % ROWS)
    return jnp.stack(slots, axis=-1).astype(jnp.int32)


def level_of(key, dims, shards, low, top_value):
    level, own = 1.0, jax.random.fold_in(key, 6)
    for position, parts in shards:
        steps = jnp.exp(jax.random.uniform(jax.random.fold_in(own, position), (parts,), jnp.float32, low / len(shards), top_value / len(shards)))
        level = level * jnp.repeat(steps, dims[position] // parts).reshape([-1 if axis == position else 1 for axis in range(len(dims))])
    return level


def noise(rng, shape, scale, limit, split=(), kind=jnp.bfloat16):
    loudness = level_of(rng, shape, split, -0.22, 0.18) if split else 1.0
    values = jax.random.normal(rng, shape, jnp.float32) * scale * loudness
    return jnp.minimum(jnp.maximum(values, -limit), limit).astype(kind)


def setup_inputs(seed: int = 0) -> dict:
    streams_of = jax.random.split(jax.random.key(seed), 8)
    return {
        "rhs": noise(streams_of[0], (N_SLAB, N_CROSS, ROWS, BLK, NV), 1.0, 6.0, ((0, 4), (1, 8))),
        "m_blocks": noise(streams_of[1], (N_SLAB, N_CROSS, EXT, NBLK, BLK, BLK), (NBLK * BLK) ** -0.5, 0.3125, ((0, 4), (1, 8))),
        "m_cols": draw_m_cols(jax.random.fold_in(streams_of[7], 71), 0),
        "j_blocks": noise(streams_of[3], (N_SLAB, N_CROSS, ROWS, NBLK, BLK, BLK), (NBLK * BLK) ** -0.5, 0.3125, ((0, 4), (1, 8))),
        "j_cols": draw_j_cols(jax.random.fold_in(streams_of[7], 71), 0),
        "send_list": draw_send_list(jax.random.fold_in(streams_of[7], 71), 0),
        "send_count": draw_send_count(jax.random.fold_in(streams_of[7], 71), 0),
    }


def extend_all(field, send_list, send_count):
    zeros = jnp.zeros_like(field[:1, :, :OVL])
    upper = jnp.concatenate([zeros, field[:-1, :, ROWS - OVL:]], axis=0)
    lower = jnp.concatenate([field[1:, :, :OVL], zeros], axis=0)
    picked = jax.vmap(jax.vmap(lambda source_rows, picks: jnp.take(source_rows, picks.reshape(-1), axis=0)))(field, send_list)
    picked = picked.reshape(N_SLAB, N_CROSS, N_CROSS, CAP, BLK, NV)
    valid = jnp.arange(CAP, dtype=jnp.int32)[None, None, None, :] < send_count[..., None]
    picked = jnp.where(valid[..., None, None], picked, jnp.zeros((), field.dtype))
    arrived = jnp.swapaxes(picked, 1, 2).reshape(N_SLAB, N_CROSS, N_CROSS * CAP, BLK, NV)
    return jnp.concatenate([field, upper, lower, arrived], axis=2)


def apply_blocks(blocks, columns, extended):
    flat_blocks = blocks.reshape((N_SLAB * N_CROSS,) + blocks.shape[2:])
    flat_cols = columns.reshape((N_SLAB * N_CROSS,) + columns.shape[2:])
    flat_ext = extended.reshape((N_SLAB * N_CROSS,) + extended.shape[2:])

    def single(items):
        block_set, col_set, ext_set = items
        gathered = jnp.take(ext_set, col_set, axis=0).astype(jnp.float32)
        return jnp.einsum('ekab,ekbn->ean', block_set.astype(jnp.float32), gathered)

    result = lax.map(single, (flat_blocks, flat_cols, flat_ext))
    return result.reshape((N_SLAB, N_CROSS) + result.shape[1:])


def assemble(partial_value, send_list, send_count):
    total = partial_value[:, :, :ROWS].astype(jnp.float32)
    upper_part = partial_value[:, :, ROWS:ROWS + OVL]
    lower_part = partial_value[:, :, ROWS + OVL:ROWS + 2 * OVL]
    zeros = jnp.zeros_like(upper_part[:1])
    from_prev = jnp.concatenate([zeros, lower_part[:-1]], axis=0).astype(jnp.float32)
    from_next = jnp.concatenate([upper_part[1:], zeros], axis=0).astype(jnp.float32)
    total = total.at[:, :, :OVL].add(from_prev)
    total = total.at[:, :, ROWS - OVL:].add(from_next)
    cross_part = partial_value[:, :, ROWS + 2 * OVL:].reshape(N_SLAB, N_CROSS, N_CROSS, CAP, BLK * NV)
    returned = jnp.swapaxes(cross_part, 1, 2).reshape(N_SLAB, N_CROSS, N_CROSS * CAP, BLK * NV).astype(jnp.float32)
    valid = (jnp.arange(CAP, dtype=jnp.int32)[None, None, None, :] < send_count[..., None]).reshape(N_SLAB, N_CROSS, N_CROSS * CAP)
    targets = send_list.reshape(N_SLAB, N_CROSS, N_CROSS * CAP)
    table = ((targets[:, :, None, :] == jnp.arange(ROWS, dtype=jnp.int32)[None, None, :, None]) & valid[:, :, None, :]).astype(jnp.float32)
    added = jnp.einsum('scrj,scjm->scrm', table, returned, precision=lax.Precision.HIGHEST)
    return total + added.reshape(N_SLAB, N_CROSS, ROWS, BLK, NV)


def precondition(field, m_blocks, m_cols, send_list, send_count):
    extended = extend_all(field, send_list, send_count)
    partial_value = apply_blocks(m_blocks, m_cols, extended).astype(jnp.bfloat16)
    return assemble(partial_value, send_list, send_count)


def reference(rhs, m_blocks, m_cols, j_blocks, j_cols, send_list, send_count):
    first = precondition(rhs, m_blocks, m_cols, send_list, send_count).astype(jnp.bfloat16)
    extended = extend_all(first, send_list, send_count)
    image = apply_blocks(j_blocks, j_cols, extended)
    residual = (rhs.astype(jnp.float32) - image).astype(jnp.bfloat16)
    second = first.astype(jnp.float32) + precondition(residual, m_blocks, m_cols, send_list, send_count)
    return second.astype(jnp.bfloat16)
```

```python
import functools

import jax
import jax.numpy as jnp
from jax import lax
from jax.experimental import pallas as pl
from jax.experimental.pallas import tpu as pltpu
from jax.sharding import PartitionSpec as P

MESH = pl.DeviceIdType.MESH
F32 = jnp.float32
BF16 = jnp.bfloat16

LENDS = 3
BACKS = 2


def kernel(
    n_slab, n, ovl, cap,
    rhs_hbm, m_hbm, j_hbm, m_cols, j_cols, targets, counts,
    out_ref,
    m_v, j_v, ext0, ext1, ext2, part, acc, run,
    lend_buf, land, lend_slab, land_slab, back_buf, ret, back_slab, ret_slab,
    prev, last, load_sem, send_sem, recv_sem,
):
    s = lax.axis_index("slab")
    c = lax.axis_index("cross")
    ext = (ext0, ext1, ext2)
    rows = part.shape[0]
    blk, nv = part.shape[1:]
    half = nv // 2
    kcount = m_v.shape[1]
    pairs = cap // 2
    opairs = ovl // 2
    base = rows + 2 * ovl
    slots = (n - 1) * cap
    zero_slot = slots
    up_i, down_i = n, n + 1
    has_up = s > 0
    has_down = s < n_slab - 1

    def peer(d):
        return lax.rem(c + d, n)

    def order(t):
        return n // 2 + (2 * lax.rem(t, 2) - 1) * ((t + 1) // 2)

    load_rhs = pltpu.make_async_copy(rhs_hbm.at[0, 0], ext0.at[pl.ds(0, rows)], load_sem.at[0])
    load_m = pltpu.make_async_copy(m_hbm.at[0, 0], m_v, load_sem.at[1])
    load_j = pltpu.make_async_copy(j_hbm.at[0, 0], j_v, load_sem.at[2])
    load_rhs.start()

    barrier = pltpu.get_barrier_semaphore()

    @pl.loop(1, n)
    def _(d):
        pl.semaphore_signal(barrier, inc=1, device_id=(s, peer(d)), device_id_type=MESH)

    @pl.when(has_up)
    def _():
        pl.semaphore_signal(barrier, inc=1, device_id=(s - 1, c), device_id_type=MESH)

    @pl.when(has_down)
    def _():
        pl.semaphore_signal(barrier, inc=1, device_id=(s + 1, c), device_id_type=MESH)

    load_m.start()
    load_j.start()


    def swap(x):
        return pltpu.roll(x, half, 1)

    def low(dtype):
        return lax.broadcasted_iota(jnp.int32, (blk, nv), 1) < half

    def pack(h, r0, r1):
        if h == 0:
            return jnp.where(low(r0.dtype), r0, swap(r1))
        return jnp.where(low(r0.dtype), swap(r0), r1)

    def apart(h, tile_of):
        a = tile_of(0)
        if h == 0:
            return a, swap(a)
        b = tile_of(1)
        mask = low(a.dtype)
        return jnp.where(mask, a, swap(b)), jnp.where(mask, swap(a), b)

    zero_tile = jnp.zeros((blk, nv), BF16)
    for e in range(LENDS):
        for t in range(cap):
            ext[e][base + c * cap + t] = zero_tile

    def clear_slab(side):
        for h in range(2):
            for u in range(opairs):
                for e in range(LENDS):
                    land_slab[e, h, side, u] = zero_tile
                for a in range(BACKS):
                    ret_slab[a, h, side, u] = zero_tile

    @pl.when(jnp.logical_not(has_up))
    def _():
        clear_slab(0)

    @pl.when(jnp.logical_not(has_down))
    def _():
        clear_slab(1)

    run[zero_slot] = jnp.zeros((blk, nv), F32)


    def cross_copy(src, dst, x, h, d):
        return pltpu.make_async_remote_copy(
            src_ref=src.at[h, d - 1], dst_ref=dst.at[h, n - d - 1],
            send_sem=send_sem.at[x, h, d], recv_sem=recv_sem.at[x, h, n - d],
            device_id=(s, peer(d)), device_id_type=MESH,
        )

    def cross_got(src, dst, x, h, d):
        return pltpu.make_async_remote_copy(
            src_ref=src.at[h, d - 1], dst_ref=dst.at[h, d - 1],
            send_sem=send_sem.at[x, h, d], recv_sem=recv_sem.at[x, h, d],
            device_id=(s, peer(d)), device_id_type=MESH,
        )

    def slab_copy(src, dst, x, h, side):
        other = 1 - side
        return pltpu.make_async_remote_copy(
            src_ref=src.at[h, side], dst_ref=dst.at[h, other],
            send_sem=send_sem.at[x, h, n + side], recv_sem=recv_sem.at[x, h, n + other],
            device_id=(s - 1 + 2 * side, c), device_id_type=MESH,
        )

    def slab_got(src, dst, x, h, side):
        return pltpu.make_async_remote_copy(
            src_ref=src.at[h, side], dst_ref=dst.at[h, side],
            send_sem=send_sem.at[x, h, n + side], recv_sem=recv_sem.at[x, h, n + side],
            device_id=(s - 1 + 2 * side, c), device_id_type=MESH,
        )

    def both_sides(do):
        @pl.when(has_up)
        def _():
            do(0)

        @pl.when(has_down)
        def _():
            do(1)

    def lend(e, h):
        src, dst = lend_buf.at[e], land.at[e]

        @pl.loop(0, n - 1)
        def _(step):
            d = order(step)
            q = peer(d)

            def picked(t):
                row = ext[e][targets[0, 0, t, q]]
                return jnp.where(t < counts[0, 0, q], row, jnp.zeros_like(row))

            for u in range(pairs):
                lend_buf[e, h, d - 1, u] = pack(h, picked(2 * u), picked(2 * u + 1))
            cross_copy(src, dst, e, h, d).start()

        for side in range(2):
            first_row = side * (rows - ovl)
            for u in range(opairs):
                r0 = first_row + 2 * u
                lend_slab[e, h, side, u] = pack(h, ext[e][r0], ext[e][r0 + 1])
        both_sides(lambda side: slab_copy(lend_slab.at[e], land_slab.at[e], e, h, side).start())

    def await_lent(e, h):
        @pl.loop(0, n - 1)
        def _(step):
            d = n - order(n - 2 - step)
            cross_got(lend_buf.at[e], land.at[e], e, h, d).wait_recv()
            for u in range(pairs):
                r0, r1 = apart(h, lambda hh: land[e, hh, d - 1, u])
                i = base + peer(d) * cap + 2 * u
                ext[e][i] = r0
                ext[e][i + 1] = r1

        both_sides(lambda side: slab_got(lend_slab.at[e], land_slab.at[e], e, h, side).wait_recv())
        for side in range(2):
            for u in range(opairs):
                r0, r1 = apart(h, lambda hh: land_slab[e, hh, side, u])
                i = rows + side * ovl + 2 * u
                ext[e][i] = r0
                ext[e][i + 1] = r1

    def row_product(blocks, cols, e, i, k0=0):
        left = jnp.concatenate([blocks[i, k] for k in range(k0, kcount)], axis=1)
        right = jnp.concatenate([ext[e][cols[0, k, 0, i]] for k in range(k0, kcount)], axis=0)
        return jnp.dot(left, right, preferred_element_type=F32)

    def give_back(a, e, h):
        x = LENDS + a

        @pl.loop(0, n - 1)
        def _(step):
            d = order(step)
            for u in range(pairs):
                i = base + peer(d) * cap + 2 * u
                tile = pack(h, row_product(m_v, m_cols, e, i), row_product(m_v, m_cols, e, i + 1))
                back_buf[a, h, d - 1, u] = tile.astype(BF16)
            cross_copy(back_buf.at[a], ret.at[a], x, h, d).start()

        for side in range(2):
            @pl.loop(0, opairs)
            def _(u):
                i = rows + side * ovl + 2 * u
                tile = pack(h, row_product(m_v, m_cols, e, i), row_product(m_v, m_cols, e, i + 1))
                back_slab[a, h, side, u] = tile.astype(BF16)

        both_sides(lambda side: slab_copy(back_slab.at[a], ret_slab.at[a], x, h, side).start())

    def own_partials(e):
        @pl.loop(0, rows // 4)
        def _(g):
            for t in range(4):
                i = 4 * g + t
                part[i] = row_product(m_v, m_cols, e, i).astype(BF16)

    def await_returns(a, h):
        x = LENDS + a

        @pl.loop(1, n)
        def _(d):
            cross_got(back_buf.at[a], ret.at[a], x, h, d).wait_recv()
            for u in range(pairs):
                two = apart(h, lambda hh: ret[a, hh, d - 1, u])
                for t in range(2):
                    p = (d - 1) * cap + 2 * u + t
                    run[p] = two[t].astype(F32) + run[prev[p]]

        both_sides(lambda side: slab_got(back_slab.at[a], ret_slab.at[a], x, h, side).wait_recv())

    def assembled(a, h, body):
        def total(i):
            return part[i].astype(F32) + run[last[i]]

        for side in range(2):
            for u in range(opairs):
                two = apart(h, lambda hh: ret_slab[a, hh, side, u])
                for t in range(2):
                    i = side * (rows - ovl) + 2 * u + t
                    body(i, total(i) + two[t].astype(F32))

        @pl.loop(0, (rows - 2 * ovl) // 4)
        def _(g):
            for t in range(4):
                i = ovl + 4 * g + t
                body(i, total(i))

    load_rhs.wait()
    pl.semaphore_wait(barrier, n - 1 + has_up.astype(jnp.int32) + has_down.astype(jnp.int32))

    lend(0, 0)
    lend(0, 1)

    def key_of(p):
        q = peer(p // cap + 1)
        t = lax.rem(p, cap)
        return jnp.where(t < counts[0, 0, q], targets[0, 0, t, q], -1)

    keys = [key_of(p) for p in range(slots)]
    for p in range(slots):
        found = zero_slot
        for p2 in range(p):
            found = jnp.where(keys[p2] == keys[p], p2, found)
        prev[p] = jnp.where(keys[p] < 0, zero_slot, found)

    @pl.loop(0, rows)
    def _(i):
        found = zero_slot
        for p in range(slots):
            found = jnp.where(keys[p] == i, p, found)
        last[i] = found

    load_m.wait()
    load_j.wait()

    await_lent(0, 0)
    give_back(0, 0, 0)
    await_lent(0, 1)
    give_back(0, 0, 1)
    own_partials(0)

    def put_first(i, value):
        ext1[i] = value.astype(BF16)

    for h in range(2):
        await_returns(0, h)
        assembled(0, h, put_first)
        lend(1, h)

    @pl.loop(0, rows // 4)
    def _(g):
        for t in range(4):
            i = 4 * g + t
            acc[i] = ext0[i].astype(F32) - jnp.dot(j_v[i, 0], ext1[i], preferred_element_type=F32)

    for h in range(2):
        await_lent(1, h)

        @pl.loop(0, rows // 4)
        def _(g):
            for t in range(4):
                i = 4 * g + t
                ext2[i] = (acc[i] - row_product(j_v, j_cols, 1, i, 1)).astype(BF16)

        lend(2, h)

    for h in range(2):
        await_lent(2, h)
        give_back(1, 2, h)

    own_partials(2)

    def put_second(i, value):
        out_ref[0, 0, i] = (ext1[i].astype(F32) + value).astype(BF16)

    both_sides(lambda side: slab_got(back_slab.at[1], ret_slab.at[1], LENDS + 1, 0, side).wait_recv())

    @pl.loop(1, n)
    def _(d):
        cross_got(back_buf.at[1], ret.at[1], LENDS + 1, 0, d).wait_recv()

    await_returns(1, 1)
    assembled(1, 1, put_second)

    for h in range(2):
        for e in range(LENDS):
            @pl.loop(1, n)
            def _(d):
                cross_copy(lend_buf.at[e], land.at[e], e, h, d).wait_send()

            both_sides(lambda side: slab_copy(lend_slab.at[e], land_slab.at[e], e, h, side).wait_send())
        for a in range(BACKS):
            @pl.loop(1, n)
            def _(d):
                cross_copy(back_buf.at[a], ret.at[a], LENDS + a, h, d).wait_send()

            both_sides(lambda side: slab_copy(back_slab.at[a], ret_slab.at[a], LENDS + a, h, side).wait_send())


def solution(mesh):
    n_slab = mesh.shape["slab"]
    n = mesh.shape["cross"]

    def per_device(rhs, m_blocks, m_cols, j_blocks, j_cols, send_list, send_count):
        rows, blk, nv = rhs.shape[2:]
        total_rows, kcount = m_blocks.shape[2:4]
        cap = send_list.shape[3]
        ovl = (total_rows - rows - n * cap) // 2
        slots = (n - 1) * cap
        tile = (blk, nv)
        smem = pl.BlockSpec(memory_space=pltpu.SMEM)
        hbm = pl.BlockSpec(memory_space=pltpu.HBM)
        return pl.pallas_call(
            functools.partial(kernel, n_slab, n, ovl, cap),
            out_shape=pltpu.VMEM(rhs.shape, rhs.dtype),
            in_specs=[hbm, hbm, hbm, smem, smem, smem, smem],
            out_specs=pl.BlockSpec(memory_space=pltpu.VMEM),
            scratch_shapes=[
                pltpu.VMEM(m_blocks.shape[2:], BF16),
                pltpu.VMEM(j_blocks.shape[2:], BF16),
                *([pltpu.VMEM((total_rows,) + tile, BF16)] * LENDS),
                pltpu.VMEM((rows,) + tile, BF16),
                pltpu.VMEM((rows,) + tile, F32),
                pltpu.VMEM((slots + 1,) + tile, F32),
                *([pltpu.VMEM((LENDS, 2, n - 1, cap // 2) + tile, BF16)] * 2),
                *([pltpu.VMEM((LENDS, 2, 2, ovl // 2) + tile, BF16)] * 2),
                *([pltpu.VMEM((BACKS, 2, n - 1, cap // 2) + tile, BF16)] * 2),
                *([pltpu.VMEM((BACKS, 2, 2, ovl // 2) + tile, BF16)] * 2),
                pltpu.SMEM((slots,), jnp.int32),
                pltpu.SMEM((rows,), jnp.int32),
                pltpu.SemaphoreType.DMA((3,)),
                pltpu.SemaphoreType.DMA((LENDS + BACKS, 2, n + 2)),
                pltpu.SemaphoreType.DMA((LENDS + BACKS, 2, n + 2)),
            ],
            compiler_params=pltpu.CompilerParams(
                collective_id=0, has_side_effects=True, vmem_limit_bytes=60 * 1024 * 1024
            ),
        )(
            rhs, m_blocks, j_blocks, m_cols.transpose(0, 3, 1, 2), j_cols.transpose(0, 3, 1, 2),
            send_list.transpose(0, 1, 3, 2), send_count,
        )

    return jax.shard_map(
        per_device,
        mesh=mesh,
        in_specs=(
            P("slab", "cross", None, None, None),
            P("slab", "cross", None, None, None, None),
            P("slab", "cross", None, None),
            P("slab", "cross", None, None, None, None),
            P("slab", "cross", None, None),
            P("slab", "cross", None, None),
            P("slab", "cross", None),
        ),
        out_specs=P("slab", "cross", None, None, None),
        check_vma=False,
    )
```

```python
import functools

import jax
import jax.numpy as jnp
from jax import lax
from jax.experimental import pallas as pl
from jax.experimental.pallas import tpu as pltpu
from jax.sharding import PartitionSpec as P

MESH = pl.DeviceIdType.MESH
F32 = jnp.float32
BF16 = jnp.bfloat16

LENDS = 3
BACKS = 2


def kernel(
    n_slab, n, ovl, cap,
    rhs_hbm, m_hbm, j_hbm, m_cols, j_cols, targets, counts,
    out_ref,
    m_v, j_v, ext0, ext1, ext2, part, acc, run,
    lend_buf, land, lend_slab, land_slab, back_buf, ret, back_slab, ret_slab,
    prev, last, load_sem, send_sem, recv_sem,
):
    s = lax.axis_index("slab")
    c = lax.axis_index("cross")
    ext = (ext0, ext1, ext2)
    rows = part.shape[0]
    blk, nv = part.shape[1:]
    half = nv // 2
    kcount = m_v.shape[1]
    pairs = cap // 2
    opairs = ovl // 2
    base = rows + 2 * ovl
    slots = (n - 1) * cap
    zero_slot = slots
    up_i, down_i = n, n + 1
    has_up = s > 0
    has_down = s < n_slab - 1

    paired = n & (n - 1) == 0
    centre = jnp.logical_and(c >= n // 4, c < n - n // 4)
    shift = jnp.where(centre, n // 2 - 1, 0)

    def peer(d):
        return jnp.bitwise_xor(c, d) if paired else lax.rem(c + d, n)

    def mirror(d):
        return d if paired else n - d

    def order(t):
        return lax.rem(t + shift, n - 1) + 1

    def grouped(do):
        do([0])
        pairs_of = (n - 2) // 2

        @pl.loop(0, pairs_of)
        def _(g):
            do([1 + 2 * g, 2 + 2 * g])

        for t in range(1 + 2 * pairs_of, n - 1):
            do([t])

    load_rhs = pltpu.make_async_copy(rhs_hbm.at[0, 0], ext0.at[pl.ds(0, rows)], load_sem.at[0])
    load_m = pltpu.make_async_copy(m_hbm.at[0, 0], m_v, load_sem.at[1])
    load_j = pltpu.make_async_copy(j_hbm.at[0, 0], j_v, load_sem.at[2])
    load_rhs.start()

    barrier = pltpu.get_barrier_semaphore()

    @pl.loop(1, n)
    def _(d):
        pl.semaphore_signal(barrier, inc=1, device_id=(s, peer(d)), device_id_type=MESH)

    @pl.when(has_up)
    def _():
        pl.semaphore_signal(barrier, inc=1, device_id=(s - 1, c), device_id_type=MESH)

    @pl.when(has_down)
    def _():
        pl.semaphore_signal(barrier, inc=1, device_id=(s + 1, c), device_id_type=MESH)

    load_m.start()
    load_j.start()


    def swap(x):
        return pltpu.roll(x, half, 1)

    def low(dtype):
        return lax.broadcasted_iota(jnp.int32, (blk, nv), 1) < half

    def pack(h, r0, r1):
        if h == 0:
            return jnp.where(low(r0.dtype), r0, swap(r1))
        return jnp.where(low(r0.dtype), swap(r0), r1)

    def apart(h, tile_of):
        a = tile_of(0)
        if h == 0:
            return a, swap(a)
        b = tile_of(1)
        mask = low(a.dtype)
        return jnp.where(mask, a, swap(b)), jnp.where(mask, swap(a), b)


    def cross_copy(src, dst, x, h, d):
        return pltpu.make_async_remote_copy(
            src_ref=src.at[h, d - 1], dst_ref=dst.at[h, mirror(d) - 1],
            send_sem=send_sem.at[x, h, 0], recv_sem=recv_sem.at[x, h, 0 if x < LENDS else mirror(d)],
            device_id=(s, peer(d)), device_id_type=MESH,
        )

    def cross_all(src, dst, x, h):
        return pltpu.make_async_remote_copy(
            src_ref=src.at[h], dst_ref=dst.at[h],
            send_sem=send_sem.at[x, h, 0], recv_sem=recv_sem.at[x, h, 0],
            device_id=(s, peer(1)), device_id_type=MESH,
        )

    def cross_got(src, dst, x, h, d):
        return pltpu.make_async_remote_copy(
            src_ref=src.at[h, d - 1], dst_ref=dst.at[h, d - 1],
            send_sem=send_sem.at[x, h, 0], recv_sem=recv_sem.at[x, h, d],
            device_id=(s, peer(d)), device_id_type=MESH,
        )

    def slab_copy(src, dst, x, h, side):
        other = 1 - side
        return pltpu.make_async_remote_copy(
            src_ref=src.at[h, side], dst_ref=dst.at[h, other],
            send_sem=send_sem.at[x, h, n + side], recv_sem=recv_sem.at[x, h, n + other],
            device_id=(s - 1 + 2 * side, c), device_id_type=MESH,
        )

    def slab_got(src, dst, x, h, side):
        return pltpu.make_async_remote_copy(
            src_ref=src.at[h, side], dst_ref=dst.at[h, side],
            send_sem=send_sem.at[x, h, n + side], recv_sem=recv_sem.at[x, h, n + side],
            device_id=(s - 1 + 2 * side, c), device_id_type=MESH,
        )

    def both_sides(do):
        @pl.when(has_up)
        def _():
            do(0)

        @pl.when(has_down)
        def _():
            do(1)

    def pack_lent(e, h, d):
        q = peer(d)

        def picked(t):
            row = ext[e][targets[0, 0, t, q]]
            return jnp.where(t < counts[0, 0, q], row, jnp.zeros_like(row))

        for u in range(pairs):
            lend_buf[e, h, d - 1, u] = pack(h, picked(2 * u), picked(2 * u + 1))

    def pack_slab(e, h):
        for side in range(2):
            first_row = side * (rows - ovl)
            for u in range(opairs):
                r0 = first_row + 2 * u
                lend_slab[e, h, side, u] = pack(h, ext[e][r0], ext[e][r0 + 1])

    def send_slab(e, h):
        both_sides(lambda side: slab_copy(lend_slab.at[e], land_slab.at[e], e, h, side).start())

    def lend(e, h):
        def some(steps):
            ds = [order(t) for t in steps]
            for d in ds:
                pack_lent(e, h, d)
            for d in ds:
                cross_copy(lend_buf.at[e], land.at[e], e, h, d).start()

        grouped(some)
        pack_slab(e, h)
        send_slab(e, h)

    def await_lent(e, h):
        both_sides(lambda side: slab_got(lend_slab.at[e], land_slab.at[e], e, h, side).wait_recv())
        for side in range(2):
            for u in range(opairs):
                r0, r1 = apart(h, lambda hh: land_slab[e, hh, side, u])
                i = rows + side * ovl + 2 * u
                ext[e][i] = r0
                ext[e][i + 1] = r1
        cross_all(lend_buf.at[e], land.at[e], e, h).wait_recv()

        def some(steps):
            for t in steps:
                d = t + 1
                for u in range(pairs):
                    r0, r1 = apart(h, lambda hh: land[e, hh, d - 1, u])
                    i = base + peer(d) * cap + 2 * u
                    ext[e][i] = r0
                    ext[e][i + 1] = r1

        grouped(some)

    def row_product(blocks, cols, e, i, k0=0):
        left = jnp.concatenate([blocks[i, k] for k in range(k0, kcount)], axis=1)
        right = jnp.concatenate([ext[e][cols[0, k, 0, i]] for k in range(k0, kcount)], axis=0)
        return jnp.dot(left, right, preferred_element_type=F32)

    def packed_product(a, e, h, i):
        return pack(h, row_product(m_v, m_cols, e, i), row_product(m_v, m_cols, e, i + 1)).astype(BF16)

    def give_back(a, e, h):
        x = LENDS + a

        def some(steps):
            ds = [order(t) for t in steps]
            for d in ds:
                for u in range(pairs):
                    back_buf[a, h, d - 1, u] = packed_product(a, e, h, base + peer(d) * cap + 2 * u)
            for d in ds:
                cross_copy(back_buf.at[a], ret.at[a], x, h, d).start()

        grouped(some)

        @pl.loop(0, 2)
        def _(side):
            for u in range(opairs):
                back_slab[a, h, side, u] = packed_product(a, e, h, rows + side * ovl + 2 * u)

        both_sides(lambda side: slab_copy(back_slab.at[a], ret_slab.at[a], x, h, side).start())

    def own_partials(e):
        @pl.loop(0, rows // 8)
        def _(g):
            for t in range(8):
                i = 8 * g + t
                part[i] = row_product(m_v, m_cols, e, i).astype(BF16)

    def await_returns(a, h):
        x = LENDS + a

        @pl.loop(1, n)
        def _(d):
            cross_got(back_buf.at[a], ret.at[a], x, h, d).wait_recv()
            for u in range(pairs):
                two = apart(h, lambda hh: ret[a, hh, d - 1, u])
                for t in range(2):
                    p = (d - 1) * cap + 2 * u + t
                    run[p] = two[t].astype(F32) + run[prev[p]]

        both_sides(lambda side: slab_got(back_slab.at[a], ret_slab.at[a], x, h, side).wait_recv())

    def assembled(a, h, body):
        def total(i):
            return part[i].astype(F32) + run[last[i]]

        for side in range(2):
            for u in range(opairs):
                two = apart(h, lambda hh: ret_slab[a, hh, side, u])
                for t in range(2):
                    i = side * (rows - ovl) + 2 * u + t
                    body(i, total(i) + two[t].astype(F32))

        @pl.loop(0, (rows - 2 * ovl) // 4)
        def _(g):
            for t in range(4):
                i = ovl + 4 * g + t
                body(i, total(i))

    load_rhs.wait()
    pl.semaphore_wait(barrier, n - 1 + has_up.astype(jnp.int32) + has_down.astype(jnp.int32))

    lend(0, 0)
    lend(0, 1)

    zero_tile = jnp.zeros((blk, nv), BF16)
    for e in range(LENDS):
        for t in range(cap):
            ext[e][base + c * cap + t] = zero_tile

    def clear_slab(side):
        for h in range(2):
            for u in range(opairs):
                for e in range(LENDS):
                    land_slab[e, h, side, u] = zero_tile
                for a in range(BACKS):
                    ret_slab[a, h, side, u] = zero_tile

    @pl.when(jnp.logical_not(has_up))
    def _():
        clear_slab(0)

    @pl.when(jnp.logical_not(has_down))
    def _():
        clear_slab(1)

    run[zero_slot] = jnp.zeros((blk, nv), F32)

    def key_of(p):
        q = peer(p // cap + 1)
        t = lax.rem(p, cap)
        return jnp.where(t < counts[0, 0, q], targets[0, 0, t, q], -1)

    keys = [key_of(p) for p in range(slots)]
    for p in range(slots):
        found = zero_slot
        for p2 in range(p):
            found = jnp.where(keys[p2] == keys[p], p2, found)
        prev[p] = jnp.where(keys[p] < 0, zero_slot, found)

    @pl.loop(0, rows)
    def _(i):
        found = zero_slot
        for p in range(slots):
            found = jnp.where(keys[p] == i, p, found)
        last[i] = found

    load_m.wait()
    load_j.wait()

    await_lent(0, 0)
    give_back(0, 0, 0)
    await_lent(0, 1)
    give_back(0, 0, 1)
    own_partials(0)

    def put_first(i, value):
        ext1[i] = value.astype(BF16)

    for h in range(2):
        await_returns(0, h)
        assembled(0, h, put_first)
        lend(1, h)

    @pl.loop(0, rows // 16)
    def _(g):
        for t in range(16):
            i = 16 * g + t
            acc[i] = ext0[i].astype(F32) - jnp.dot(j_v[i, 0], ext1[i], preferred_element_type=F32)

    for h in range(2):
        await_lent(1, h)

        @pl.loop(0, rows // 16)
        def _(g):
            for t in range(16):
                i = 16 * g + t
                ext2[i] = (acc[i] - row_product(j_v, j_cols, 1, i, 1)).astype(BF16)

        lend(2, h)

    for h in range(2):
        await_lent(2, h)
        give_back(1, 2, h)

    own_partials(2)

    def put_second(i, value):
        out_ref[0, 0, i] = (ext1[i].astype(F32) + value).astype(BF16)

    def sent(src, dst, src_slab, dst_slab, x, h):
        cross_all(src, dst, x, h).wait_send()
        both_sides(lambda side: slab_copy(src_slab, dst_slab, x, h, side).wait_send())

    for h in range(2):
        for e in range(LENDS):
            sent(lend_buf.at[e], land.at[e], lend_slab.at[e], land_slab.at[e], e, h)
        for a in range(BACKS):
            sent(back_buf.at[a], ret.at[a], back_slab.at[a], ret_slab.at[a], LENDS + a, h)

    both_sides(lambda side: slab_got(back_slab.at[1], ret_slab.at[1], LENDS + 1, 0, side).wait_recv())

    @pl.loop(1, n)
    def _(d):
        cross_got(back_buf.at[1], ret.at[1], LENDS + 1, 0, d).wait_recv()

    await_returns(1, 1)
    assembled(1, 1, put_second)


def solution(mesh):
    n_slab = mesh.shape["slab"]
    n = mesh.shape["cross"]

    def per_device(rhs, m_blocks, m_cols, j_blocks, j_cols, send_list, send_count):
        rows, blk, nv = rhs.shape[2:]
        total_rows, kcount = m_blocks.shape[2:4]
        cap = send_list.shape[3]
        ovl = (total_rows - rows - n * cap) // 2
        slots = (n - 1) * cap
        tile = (blk, nv)
        smem = pl.BlockSpec(memory_space=pltpu.SMEM)
        hbm = pl.BlockSpec(memory_space=pltpu.HBM)
        return pl.pallas_call(
            functools.partial(kernel, n_slab, n, ovl, cap),
            out_shape=pltpu.VMEM(rhs.shape, rhs.dtype),
            in_specs=[hbm, hbm, hbm, smem, smem, smem, smem],
            out_specs=pl.BlockSpec(memory_space=pltpu.VMEM),
            scratch_shapes=[
                pltpu.VMEM(m_blocks.shape[2:], BF16),
                pltpu.VMEM(j_blocks.shape[2:], BF16),
                *([pltpu.VMEM((total_rows,) + tile, BF16)] * LENDS),
                pltpu.VMEM((rows,) + tile, BF16),
                pltpu.VMEM((rows,) + tile, F32),
                pltpu.VMEM((slots + 1,) + tile, F32),
                *([pltpu.VMEM((LENDS, 2, n - 1, cap // 2) + tile, BF16)] * 2),
                *([pltpu.VMEM((LENDS, 2, 2, ovl // 2) + tile, BF16)] * 2),
                *([pltpu.VMEM((BACKS, 2, n - 1, cap // 2) + tile, BF16)] * 2),
                *([pltpu.VMEM((BACKS, 2, 2, ovl // 2) + tile, BF16)] * 2),
                pltpu.SMEM((slots,), jnp.int32),
                pltpu.SMEM((rows,), jnp.int32),
                pltpu.SemaphoreType.DMA((3,)),
                pltpu.SemaphoreType.DMA((LENDS + BACKS, 2, n + 2)),
                pltpu.SemaphoreType.DMA((LENDS + BACKS, 2, n + 2)),
            ],
            compiler_params=pltpu.CompilerParams(
                collective_id=0, has_side_effects=True, vmem_limit_bytes=60 * 1024 * 1024
            ),
        )(
            rhs, m_blocks, j_blocks, m_cols.transpose(0, 3, 1, 2), j_cols.transpose(0, 3, 1, 2),
            send_list.transpose(0, 1, 3, 2), send_count,
        )

    return jax.shard_map(
        per_device,
        mesh=mesh,
        in_specs=(
            P("slab", "cross", None, None, None),
            P("slab", "cross", None, None, None, None),
            P("slab", "cross", None, None),
            P("slab", "cross", None, None, None, None),
            P("slab", "cross", None, None),
            P("slab", "cross", None, None),
            P("slab", "cross", None),
        ),
        out_specs=P("slab", "cross", None, None, None),
        check_vma=False,
    )
```

```python
import functools

import jax
import jax.numpy as jnp
from jax import lax
from jax.experimental import pallas as pl
from jax.experimental.pallas import tpu as pltpu
from jax.sharding import PartitionSpec as P

MESH = pl.DeviceIdType.MESH
F32 = jnp.float32
BF16 = jnp.bfloat16

LENDS = 3
BACKS = 2


def kernel(
    n_slab, n, ovl, cap,
    rhs_hbm, m_hbm, j_hbm, m_cols, j_cols, targets, counts,
    out_ref,
    m_v, j_v, ext0, ext1, ext2, part, acc, run,
    lend_buf, land, lend_slab, land_slab, back_buf, ret, back_slab, ret_slab,
    prev, last, load_sem, send_sem, recv_sem, ends_in, rest_in, down_in,
):
    s = lax.axis_index("slab")
    c = lax.axis_index("cross")
    ext = (ext0, ext1, ext2)
    rows = part.shape[0]
    blk, nv = part.shape[1:]
    half = nv // 2
    kcount = m_v.shape[1]
    pairs = cap // 2
    opairs = ovl // 2
    base = rows + 2 * ovl
    slots = (n - 1) * cap
    zero_slot = slots
    up_i, down_i = n, n + 1
    has_up = s > 0
    has_down = s < n_slab - 1

    assert n >= 4 and n & (n - 1) == 0
    centre = jnp.logical_and(c >= n // 4, c < n - n // 4)
    shift = jnp.where(centre, n // 2 - 1, 0)

    def peer(d):
        return jnp.bitwise_xor(c, d)

    def order(t):
        return lax.rem(t + shift, n - 1) + 1

    def grouped(do):
        do([0])
        pairs_of = (n - 2) // 2

        @pl.loop(0, pairs_of)
        def _(g):
            do([1 + 2 * g, 2 + 2 * g])

        for t in range(1 + 2 * pairs_of, n - 1):
            do([t])

    load_rhs = pltpu.make_async_copy(rhs_hbm.at[0, 0], ext0.at[pl.ds(0, rows)], load_sem.at[0])
    load_m = pltpu.make_async_copy(m_hbm.at[0, 0], m_v, load_sem.at[1])
    load_j = pltpu.make_async_copy(j_hbm.at[0, 0], j_v, load_sem.at[2])
    load_rhs.start()

    barrier = pltpu.get_barrier_semaphore()

    def greet(sem, to_slab, to_cross):
        pl.semaphore_signal(sem, inc=1, device_id=(to_slab, to_cross), device_id_type=MESH)

    quarter = n // 4
    centre_first = quarter
    centre_count = n // 2

    @pl.when(centre)
    def _():
        @pl.loop(1, n)
        def _(d):
            greet(barrier, s, lax.rem(c + d, n))

    @pl.when(has_down)
    def _():
        greet(barrier, s + 1, c)

    def pass_barrier():
        expected = centre_count - centre.astype(jnp.int32) + has_up.astype(jnp.int32)
        pl.semaphore_wait(barrier, expected)

        @pl.when(jnp.logical_not(centre))
        def _():
            @pl.loop(centre_first, centre_first + centre_count)
            def _(q):
                greet(ends_in, s, q)

        @pl.when(has_up)
        def _():
            greet(down_in, s - 1, c)

    def hear_ends():
        pl.semaphore_wait(ends_in, n - centre_count)
        greet(rest_in, s, jnp.where(c < n // 2, c - quarter, c + quarter))

    load_m.start()
    load_j.start()


    def swap(x):
        return pltpu.roll(x, half, 1)

    def low(dtype):
        return lax.broadcasted_iota(jnp.int32, (blk, nv), 1) < half

    def pack(h, r0, r1):
        if h == 0:
            return jnp.where(low(r0.dtype), r0, swap(r1))
        return jnp.where(low(r0.dtype), swap(r0), r1)

    def apart(h, tile_of):
        a = tile_of(0)
        if h == 0:
            return a, swap(a)
        b = tile_of(1)
        mask = low(a.dtype)
        return jnp.where(mask, a, swap(b)), jnp.where(mask, swap(a), b)


    def cross_copy(src, dst, x, h, d):
        return pltpu.make_async_remote_copy(
            src_ref=src.at[h, d - 1], dst_ref=dst.at[h, d - 1],
            send_sem=send_sem.at[x, h, 0], recv_sem=recv_sem.at[x, h, 0 if x < LENDS else d],
            device_id=(s, peer(d)), device_id_type=MESH,
        )

    def cross_all(src, dst, x, h):
        return pltpu.make_async_remote_copy(
            src_ref=src.at[h], dst_ref=dst.at[h],
            send_sem=send_sem.at[x, h, 0], recv_sem=recv_sem.at[x, h, 0],
            device_id=(s, peer(1)), device_id_type=MESH,
        )

    def cross_got(src, dst, x, h, d):
        return pltpu.make_async_remote_copy(
            src_ref=src.at[h, d - 1], dst_ref=dst.at[h, d - 1],
            send_sem=send_sem.at[x, h, 0], recv_sem=recv_sem.at[x, h, d],
            device_id=(s, peer(d)), device_id_type=MESH,
        )

    def slab_copy(src, dst, x, h, side):
        other = 1 - side
        return pltpu.make_async_remote_copy(
            src_ref=src.at[h, side], dst_ref=dst.at[h, other],
            send_sem=send_sem.at[x, h, n + side], recv_sem=recv_sem.at[x, h, n + other],
            device_id=(s - 1 + 2 * side, c), device_id_type=MESH,
        )

    def slab_got(src, dst, x, h, side):
        return pltpu.make_async_remote_copy(
            src_ref=src.at[h, side], dst_ref=dst.at[h, side],
            send_sem=send_sem.at[x, h, n + side], recv_sem=recv_sem.at[x, h, n + side],
            device_id=(s - 1 + 2 * side, c), device_id_type=MESH,
        )

    def both_sides(do):
        @pl.when(has_up)
        def _():
            do(0)

        @pl.when(has_down)
        def _():
            do(1)

    def pack_lent(e, h, d):
        q = peer(d)

        def picked(t):
            row = ext[e][targets[0, 0, t, q]]
            return jnp.where(t < counts[0, 0, q], row, jnp.zeros_like(row))

        for u in range(pairs):
            lend_buf[e, h, d - 1, u] = pack(h, picked(2 * u), picked(2 * u + 1))

    def pack_slab(e, h):
        for side in range(2):
            first_row = side * (rows - ovl)
            for u in range(opairs):
                r0 = first_row + 2 * u
                lend_slab[e, h, side, u] = pack(h, ext[e][r0], ext[e][r0 + 1])

    def send_slab(e, h):
        both_sides(lambda side: slab_copy(lend_slab.at[e], land_slab.at[e], e, h, side).start())

    def lend(e, h):
        def some(steps):
            ds = [order(t) for t in steps]
            for d in ds:
                pack_lent(e, h, d)
            for d in ds:
                cross_copy(lend_buf.at[e], land.at[e], e, h, d).start()

        grouped(some)
        pack_slab(e, h)
        send_slab(e, h)

    def await_lent(e, h):
        both_sides(lambda side: slab_got(lend_slab.at[e], land_slab.at[e], e, h, side).wait_recv())
        for side in range(2):
            for u in range(opairs):
                r0, r1 = apart(h, lambda hh: land_slab[e, hh, side, u])
                i = rows + side * ovl + 2 * u
                ext[e][i] = r0
                ext[e][i + 1] = r1
        cross_all(lend_buf.at[e], land.at[e], e, h).wait_recv()

        def some(steps):
            for t in steps:
                d = t + 1
                for u in range(pairs):
                    r0, r1 = apart(h, lambda hh: land[e, hh, d - 1, u])
                    i = base + peer(d) * cap + 2 * u
                    ext[e][i] = r0
                    ext[e][i + 1] = r1

        grouped(some)

    def row_product(blocks, cols, e, i, k0=0):
        left = jnp.concatenate([blocks[i, k] for k in range(k0, kcount)], axis=1)
        right = jnp.concatenate([ext[e][cols[0, k, 0, i]] for k in range(k0, kcount)], axis=0)
        return jnp.dot(left, right, preferred_element_type=F32)

    def packed_product(a, e, h, i):
        return pack(h, row_product(m_v, m_cols, e, i), row_product(m_v, m_cols, e, i + 1)).astype(BF16)

    def give_back(a, e, h):
        x = LENDS + a

        def some(steps):
            ds = [order(t) for t in steps]
            for d in ds:
                for u in range(pairs):
                    back_buf[a, h, d - 1, u] = packed_product(a, e, h, base + peer(d) * cap + 2 * u)
            for d in ds:
                cross_copy(back_buf.at[a], ret.at[a], x, h, d).start()

        grouped(some)

        @pl.loop(0, 2)
        def _(side):
            for u in range(opairs):
                back_slab[a, h, side, u] = packed_product(a, e, h, rows + side * ovl + 2 * u)

        both_sides(lambda side: slab_copy(back_slab.at[a], ret_slab.at[a], x, h, side).start())

    def own_partials(e):
        @pl.loop(0, rows // 8)
        def _(g):
            for t in range(8):
                i = 8 * g + t
                part[i] = row_product(m_v, m_cols, e, i).astype(BF16)

    def await_returns(a, h):
        x = LENDS + a

        @pl.loop(1, n)
        def _(d):
            cross_got(back_buf.at[a], ret.at[a], x, h, d).wait_recv()
            for u in range(pairs):
                two = apart(h, lambda hh: ret[a, hh, d - 1, u])
                for t in range(2):
                    p = (d - 1) * cap + 2 * u + t
                    run[p] = two[t].astype(F32) + run[prev[p]]

        both_sides(lambda side: slab_got(back_slab.at[a], ret_slab.at[a], x, h, side).wait_recv())

    def assembled(a, h, body):
        def total(i):
            return part[i].astype(F32) + run[last[i]]

        for side in range(2):
            for u in range(opairs):
                two = apart(h, lambda hh: ret_slab[a, hh, side, u])
                for t in range(2):
                    i = side * (rows - ovl) + 2 * u + t
                    body(i, total(i) + two[t].astype(F32))

        @pl.loop(0, (rows - 2 * ovl) // 4)
        def _(g):
            for t in range(4):
                i = ovl + 4 * g + t
                body(i, total(i))

    load_rhs.wait()
    pass_barrier()

    def lend_some(h, low_d, high_d):
        @pl.loop(low_d, high_d)
        def _(d):
            pack_lent(0, h, d)
            cross_copy(lend_buf.at[0], land.at[0], 0, h, d).start()


    @pl.when(centre)
    def _():
        lend_some(0, 3 * quarter, n)
        lend_some(1, 3 * quarter, n)
        hear_ends()
        for h in range(2):
            lend_some(h, 2 * quarter, 3 * quarter)
            lend_some(h, 1, 2 * quarter)

    @pl.when(jnp.logical_not(centre))
    def _():
        lend_some(0, quarter, 3 * quarter)
        pl.semaphore_wait(rest_in, 1)
        lend_some(0, 3 * quarter, n)
        lend_some(0, 1, quarter)
        lend_some(1, quarter, n)
        lend_some(1, 1, quarter)

    @pl.when(has_down)
    def _():
        pl.semaphore_wait(down_in, 1)

    for h in range(2):
        pack_slab(0, h)
        send_slab(0, h)

    zero_tile = jnp.zeros((blk, nv), BF16)
    for e in range(LENDS):
        for t in range(cap):
            ext[e][base + c * cap + t] = zero_tile

    def clear_slab(side):
        for h in range(2):
            for u in range(opairs):
                for e in range(LENDS):
                    land_slab[e, h, side, u] = zero_tile
                for a in range(BACKS):
                    ret_slab[a, h, side, u] = zero_tile

    @pl.when(jnp.logical_not(has_up))
    def _():
        clear_slab(0)

    @pl.when(jnp.logical_not(has_down))
    def _():
        clear_slab(1)

    run[zero_slot] = jnp.zeros((blk, nv), F32)

    def key_of(p):
        q = peer(p // cap + 1)
        t = lax.rem(p, cap)
        return jnp.where(t < counts[0, 0, q], targets[0, 0, t, q], -1)

    keys = [key_of(p) for p in range(slots)]
    for p in range(slots):
        found = zero_slot
        for p2 in range(p):
            found = jnp.where(keys[p2] == keys[p], p2, found)
        prev[p] = jnp.where(keys[p] < 0, zero_slot, found)

    @pl.loop(0, rows)
    def _(i):
        found = zero_slot
        for p in range(slots):
            found = jnp.where(keys[p] == i, p, found)
        last[i] = found

    load_m.wait()
    load_j.wait()

    await_lent(0, 0)
    give_back(0, 0, 0)
    await_lent(0, 1)
    give_back(0, 0, 1)
    own_partials(0)

    def put_first(i, value):
        ext1[i] = value.astype(BF16)

    for h in range(2):
        await_returns(0, h)
        assembled(0, h, put_first)
        lend(1, h)

    @pl.loop(0, rows // 16)
    def _(g):
        for t in range(16):
            i = 16 * g + t
            acc[i] = ext0[i].astype(F32) - jnp.dot(j_v[i, 0], ext1[i], preferred_element_type=F32)

    for h in range(2):
        await_lent(1, h)

        @pl.loop(0, rows // 16)
        def _(g):
            for t in range(16):
                i = 16 * g + t
                ext2[i] = (acc[i] - row_product(j_v, j_cols, 1, i, 1)).astype(BF16)

        lend(2, h)

    for h in range(2):
        await_lent(2, h)
        give_back(1, 2, h)

    own_partials(2)

    def put_second(i, value):
        out_ref[0, 0, i] = (ext1[i].astype(F32) + value).astype(BF16)

    def sent(src, dst, src_slab, dst_slab, x, h):
        cross_all(src, dst, x, h).wait_send()
        both_sides(lambda side: slab_copy(src_slab, dst_slab, x, h, side).wait_send())

    for h in range(2):
        for e in range(LENDS):
            sent(lend_buf.at[e], land.at[e], lend_slab.at[e], land_slab.at[e], e, h)
        for a in range(BACKS):
            sent(back_buf.at[a], ret.at[a], back_slab.at[a], ret_slab.at[a], LENDS + a, h)

    both_sides(lambda side: slab_got(back_slab.at[1], ret_slab.at[1], LENDS + 1, 0, side).wait_recv())

    @pl.loop(1, n)
    def _(d):
        cross_got(back_buf.at[1], ret.at[1], LENDS + 1, 0, d).wait_recv()

    await_returns(1, 1)
    assembled(1, 1, put_second)


def solution(mesh):
    n_slab = mesh.shape["slab"]
    n = mesh.shape["cross"]

    def per_device(rhs, m_blocks, m_cols, j_blocks, j_cols, send_list, send_count):
        rows, blk, nv = rhs.shape[2:]
        total_rows, kcount = m_blocks.shape[2:4]
        cap = send_list.shape[3]
        ovl = (total_rows - rows - n * cap) // 2
        slots = (n - 1) * cap
        tile = (blk, nv)
        smem = pl.BlockSpec(memory_space=pltpu.SMEM)
        hbm = pl.BlockSpec(memory_space=pltpu.HBM)
        return pl.pallas_call(
            functools.partial(kernel, n_slab, n, ovl, cap),
            out_shape=pltpu.VMEM(rhs.shape, rhs.dtype),
            in_specs=[hbm, hbm, hbm, smem, smem, smem, smem],
            out_specs=pl.BlockSpec(memory_space=pltpu.VMEM),
            scratch_shapes=[
                pltpu.VMEM(m_blocks.shape[2:], BF16),
                pltpu.VMEM(j_blocks.shape[2:], BF16),
                *([pltpu.VMEM((total_rows,) + tile, BF16)] * LENDS),
                pltpu.VMEM((rows,) + tile, BF16),
                pltpu.VMEM((rows,) + tile, F32),
                pltpu.VMEM((slots + 1,) + tile, F32),
                *([pltpu.VMEM((LENDS, 2, n - 1, cap // 2) + tile, BF16)] * 2),
                *([pltpu.VMEM((LENDS, 2, 2, ovl // 2) + tile, BF16)] * 2),
                *([pltpu.VMEM((BACKS, 2, n - 1, cap // 2) + tile, BF16)] * 2),
                *([pltpu.VMEM((BACKS, 2, 2, ovl // 2) + tile, BF16)] * 2),
                pltpu.SMEM((slots,), jnp.int32),
                pltpu.SMEM((rows,), jnp.int32),
                pltpu.SemaphoreType.DMA((3,)),
                pltpu.SemaphoreType.DMA((LENDS + BACKS, 2, n + 2)),
                pltpu.SemaphoreType.DMA((LENDS + BACKS, 2, n + 2)),
                pltpu.SemaphoreType.REGULAR,
                pltpu.SemaphoreType.REGULAR,
                pltpu.SemaphoreType.REGULAR,
            ],
            compiler_params=pltpu.CompilerParams(
                collective_id=0, has_side_effects=True, vmem_limit_bytes=60 * 1024 * 1024
            ),
        )(
            rhs, m_blocks, j_blocks, m_cols.transpose(0, 3, 1, 2), j_cols.transpose(0, 3, 1, 2),
            send_list.transpose(0, 1, 3, 2), send_count,
        )

    return jax.shard_map(
        per_device,
        mesh=mesh,
        in_specs=(
            P("slab", "cross", None, None, None),
            P("slab", "cross", None, None, None, None),
            P("slab", "cross", None, None),
            P("slab", "cross", None, None, None, None),
            P("slab", "cross", None, None),
            P("slab", "cross", None, None),
            P("slab", "cross", None),
        ),
        out_specs=P("slab", "cross", None, None, None),
        check_vma=False,
    )
```

```python
import functools

import jax
import jax.numpy as jnp
from jax import lax
from jax.experimental import pallas as pl
from jax.experimental.pallas import tpu as pltpu
from jax.sharding import PartitionSpec as P

MESH = pl.DeviceIdType.MESH
F32 = jnp.float32
BF16 = jnp.bfloat16

LENDS = 3
BACKS = 2


def kernel(
    n_slab, n, ovl, cap,
    rhs_hbm, m_hbm, j_hbm, m_cols, j_cols, targets, counts,
    out_ref,
    m_v, j_v, ext0, ext1, ext2, part, acc, run,
    lend_buf, land, lend_slab, land_slab, back_buf, ret, back_slab, ret_slab,
    prev, last, load_sem, send_sem, recv_sem, ends_in, rest_in, down_in,
):
    s = lax.axis_index("slab")
    c = lax.axis_index("cross")
    ext = (ext0, ext1, ext2)
    rows = part.shape[0]
    blk, nv = part.shape[1:]
    half = nv // 2
    kcount = m_v.shape[1]
    pairs = cap // 2
    opairs = ovl // 2
    base = rows + 2 * ovl
    slots = (n - 1) * cap
    zero_slot = slots
    up_i, down_i = n, n + 1
    has_up = s > 0
    has_down = s < n_slab - 1

    assert n >= 4 and n & (n - 1) == 0
    centre = jnp.logical_and(c >= n // 4, c < n - n // 4)
    shift = jnp.where(centre, n // 2 - 1, 0)

    def peer(d):
        return jnp.bitwise_xor(c, d)

    def order(t, shift=shift):
        return lax.rem(t + shift, n - 1) + 1

    last_shift = jnp.where(centre, 2 * (n // 4) - 1, 3 * (n // 4) - 1)

    def grouped(do):
        do([0])
        pairs_of = (n - 2) // 2

        @pl.loop(0, pairs_of)
        def _(g):
            do([1 + 2 * g, 2 + 2 * g])

        for t in range(1 + 2 * pairs_of, n - 1):
            do([t])

    load_rhs = pltpu.make_async_copy(rhs_hbm.at[0, 0], ext0.at[pl.ds(0, rows)], load_sem.at[0])
    load_m = pltpu.make_async_copy(m_hbm.at[0, 0], m_v, load_sem.at[1])
    load_j = pltpu.make_async_copy(j_hbm.at[0, 0], j_v, load_sem.at[2])
    load_rhs.start()

    barrier = pltpu.get_barrier_semaphore()

    def greet(sem, to_slab, to_cross):
        pl.semaphore_signal(sem, inc=1, device_id=(to_slab, to_cross), device_id_type=MESH)

    quarter = n // 4
    centre_first = quarter
    centre_count = n // 2

    @pl.when(centre)
    def _():
        @pl.loop(1, n)
        def _(d):
            greet(barrier, s, lax.rem(c + d, n))

    @pl.when(has_down)
    def _():
        greet(barrier, s + 1, c)

    def pass_barrier():
        expected = centre_count - centre.astype(jnp.int32) + has_up.astype(jnp.int32)
        pl.semaphore_wait(barrier, expected)

        @pl.when(jnp.logical_not(centre))
        def _():
            @pl.loop(centre_first, centre_first + centre_count)
            def _(q):
                greet(ends_in, s, q)

        @pl.when(has_up)
        def _():
            greet(down_in, s - 1, c)

    def hear_ends():
        pl.semaphore_wait(ends_in, n - centre_count)
        greet(rest_in, s, jnp.where(c < n // 2, c - quarter, c + quarter))


    def swap(x):
        return pltpu.roll(x, half, 1)

    def low(dtype):
        return lax.broadcasted_iota(jnp.int32, (blk, nv), 1) < half

    def pack(h, r0, r1):
        if h == 0:
            return jnp.where(low(r0.dtype), r0, swap(r1))
        return jnp.where(low(r0.dtype), swap(r0), r1)

    def apart(h, tile_of):
        a = tile_of(0)
        if h == 0:
            return a, swap(a)
        b = tile_of(1)
        mask = low(a.dtype)
        return jnp.where(mask, a, swap(b)), jnp.where(mask, swap(a), b)


    def cross_copy(src, dst, x, h, d):
        return pltpu.make_async_remote_copy(
            src_ref=src.at[h, d - 1], dst_ref=dst.at[h, d - 1],
            send_sem=send_sem.at[x, h, 0], recv_sem=recv_sem.at[x, h, 0 if x < LENDS else d],
            device_id=(s, peer(d)), device_id_type=MESH,
        )

    def cross_all(src, dst, x, h):
        return pltpu.make_async_remote_copy(
            src_ref=src.at[h], dst_ref=dst.at[h],
            send_sem=send_sem.at[x, h, 0], recv_sem=recv_sem.at[x, h, 0],
            device_id=(s, peer(1)), device_id_type=MESH,
        )

    def cross_got(src, dst, x, h, d):
        return pltpu.make_async_remote_copy(
            src_ref=src.at[h, d - 1], dst_ref=dst.at[h, d - 1],
            send_sem=send_sem.at[x, h, 0], recv_sem=recv_sem.at[x, h, d],
            device_id=(s, peer(d)), device_id_type=MESH,
        )

    def slab_copy(src, dst, x, h, side):
        other = 1 - side
        return pltpu.make_async_remote_copy(
            src_ref=src.at[h, side], dst_ref=dst.at[h, other],
            send_sem=send_sem.at[x, h, n + side], recv_sem=recv_sem.at[x, h, n + other],
            device_id=(s - 1 + 2 * side, c), device_id_type=MESH,
        )

    def slab_got(src, dst, x, h, side):
        return pltpu.make_async_remote_copy(
            src_ref=src.at[h, side], dst_ref=dst.at[h, side],
            send_sem=send_sem.at[x, h, n + side], recv_sem=recv_sem.at[x, h, n + side],
            device_id=(s - 1 + 2 * side, c), device_id_type=MESH,
        )

    def both_sides(do):
        @pl.when(has_up)
        def _():
            do(0)

        @pl.when(has_down)
        def _():
            do(1)

    def pack_lent(e, h, d):
        q = peer(d)

        def picked(t):
            row = ext[e][targets[0, 0, t, q]]
            return jnp.where(t < counts[0, 0, q], row, jnp.zeros_like(row))

        for u in range(pairs):
            lend_buf[e, h, d - 1, u] = pack(h, picked(2 * u), picked(2 * u + 1))

    def pack_slab(e, h):
        for side in range(2):
            first_row = side * (rows - ovl)
            for u in range(opairs):
                r0 = first_row + 2 * u
                lend_slab[e, h, side, u] = pack(h, ext[e][r0], ext[e][r0 + 1])

    def send_slab(e, h):
        both_sides(lambda side: slab_copy(lend_slab.at[e], land_slab.at[e], e, h, side).start())

    def lend(e, h):
        def some(steps):
            ds = [order(t) for t in steps]
            for d in ds:
                pack_lent(e, h, d)
            for d in ds:
                cross_copy(lend_buf.at[e], land.at[e], e, h, d).start()

        grouped(some)
        pack_slab(e, h)
        send_slab(e, h)

    def await_lent(e, h):
        both_sides(lambda side: slab_got(lend_slab.at[e], land_slab.at[e], e, h, side).wait_recv())
        for side in range(2):
            for u in range(opairs):
                r0, r1 = apart(h, lambda hh: land_slab[e, hh, side, u])
                i = rows + side * ovl + 2 * u
                ext[e][i] = r0
                ext[e][i + 1] = r1
        cross_all(lend_buf.at[e], land.at[e], e, h).wait_recv()

        def some(steps):
            for t in steps:
                d = t + 1
                for u in range(pairs):
                    r0, r1 = apart(h, lambda hh: land[e, hh, d - 1, u])
                    i = base + peer(d) * cap + 2 * u
                    ext[e][i] = r0
                    ext[e][i + 1] = r1

        grouped(some)

    def row_product(blocks, cols, e, i, k0=0):
        left = jnp.concatenate([blocks[i, k] for k in range(k0, kcount)], axis=1)
        right = jnp.concatenate([ext[e][cols[0, k, 0, i]] for k in range(k0, kcount)], axis=0)
        return jnp.dot(left, right, preferred_element_type=F32)

    def packed_product(a, e, h, i):
        return pack(h, row_product(m_v, m_cols, e, i), row_product(m_v, m_cols, e, i + 1)).astype(BF16)

    def give_back(a, e, h):
        x = LENDS + a

        def some(steps):
            ds = [order(t, last_shift if a == 1 else shift) for t in steps]
            for d in ds:
                for u in range(pairs):
                    back_buf[a, h, d - 1, u] = packed_product(a, e, h, base + peer(d) * cap + 2 * u)
            for d in ds:
                cross_copy(back_buf.at[a], ret.at[a], x, h, d).start()

        grouped(some)

        @pl.loop(0, 2)
        def _(side):
            for u in range(opairs):
                back_slab[a, h, side, u] = packed_product(a, e, h, rows + side * ovl + 2 * u)

        both_sides(lambda side: slab_copy(back_slab.at[a], ret_slab.at[a], x, h, side).start())

    def own_partials(e):
        @pl.loop(0, rows // 8)
        def _(g):
            for t in range(8):
                i = 8 * g + t
                part[i] = row_product(m_v, m_cols, e, i).astype(BF16)

    def chain_returns(a, h):
        x = LENDS + a

        @pl.loop(1, n)
        def _(d):
            cross_got(back_buf.at[a], ret.at[a], x, h, d).wait_recv()
            for u in range(pairs):
                two = apart(h, lambda hh: ret[a, hh, d - 1, u])
                for t in range(2):
                    p = (d - 1) * cap + 2 * u + t
                    run[p] = two[t].astype(F32) + run[prev[p]]

    def await_returns(a, h):
        chain_returns(a, h)
        both_sides(lambda side: slab_got(back_slab.at[a], ret_slab.at[a], LENDS + a, h, side).wait_recv())

    def assembled(a, h, body):
        def total(i):
            return part[i].astype(F32) + run[last[i]]

        for side in range(2):
            for u in range(opairs):
                two = apart(h, lambda hh: ret_slab[a, hh, side, u])
                for t in range(2):
                    i = side * (rows - ovl) + 2 * u + t
                    body(i, total(i) + two[t].astype(F32))

        @pl.loop(0, (rows - 2 * ovl) // 4)
        def _(g):
            for t in range(4):
                i = ovl + 4 * g + t
                body(i, total(i))

    pass_barrier()
    load_rhs.wait()
    load_m.start()
    load_j.start()

    def lend_some(h, low_d, high_d):
        @pl.loop(low_d, high_d)
        def _(d):
            pack_lent(0, h, d)
            cross_copy(lend_buf.at[0], land.at[0], 0, h, d).start()


    @pl.when(centre)
    def _():
        lend_some(0, 3 * quarter, n)
        lend_some(1, 3 * quarter, n)
        hear_ends()
        for h in range(2):
            lend_some(h, 2 * quarter, 3 * quarter)
            lend_some(h, 1, 2 * quarter)

    @pl.when(jnp.logical_not(centre))
    def _():
        lend_some(0, quarter, 3 * quarter)
        pl.semaphore_wait(rest_in, 1)
        lend_some(0, 3 * quarter, n)
        lend_some(0, 1, quarter)
        lend_some(1, quarter, n)
        lend_some(1, 1, quarter)

    @pl.when(has_down)
    def _():
        pl.semaphore_wait(down_in, 1)

    for h in range(2):
        pack_slab(0, h)
        send_slab(0, h)

    zero_tile = jnp.zeros((blk, nv), BF16)
    for e in range(LENDS):
        for t in range(cap):
            ext[e][base + c * cap + t] = zero_tile

    def clear_slab(side):
        for h in range(2):
            for u in range(opairs):
                for e in range(LENDS):
                    land_slab[e, h, side, u] = zero_tile
                for a in range(BACKS):
                    ret_slab[a, h, side, u] = zero_tile

    @pl.when(jnp.logical_not(has_up))
    def _():
        clear_slab(0)

    @pl.when(jnp.logical_not(has_down))
    def _():
        clear_slab(1)

    run[zero_slot] = jnp.zeros((blk, nv), F32)

    def key_of(p):
        q = peer(p // cap + 1)
        t = lax.rem(p, cap)
        return jnp.where(t < counts[0, 0, q], targets[0, 0, t, q], -1)

    keys = [key_of(p) for p in range(slots)]
    for p in range(slots):
        found = zero_slot
        for p2 in range(p):
            found = jnp.where(keys[p2] == keys[p], p2, found)
        prev[p] = jnp.where(keys[p] < 0, zero_slot, found)

    @pl.loop(0, rows)
    def _(i):
        found = zero_slot
        for p in range(slots):
            found = jnp.where(keys[p] == i, p, found)
        last[i] = found

    load_m.wait()
    load_j.wait()

    await_lent(0, 0)
    give_back(0, 0, 0)
    await_lent(0, 1)
    give_back(0, 0, 1)
    own_partials(0)

    def put_first(i, value):
        ext1[i] = value.astype(BF16)

    for h in range(2):
        await_returns(0, h)
        assembled(0, h, put_first)
        lend(1, h)

    @pl.loop(0, rows // 16)
    def _(g):
        for t in range(16):
            i = 16 * g + t
            acc[i] = ext0[i].astype(F32) - jnp.dot(j_v[i, 0], ext1[i], preferred_element_type=F32)

    for h in range(2):
        await_lent(1, h)

        @pl.loop(0, rows // 16)
        def _(g):
            for t in range(16):
                i = 16 * g + t
                ext2[i] = (acc[i] - row_product(j_v, j_cols, 1, i, 1)).astype(BF16)

        lend(2, h)

    for h in range(2):
        await_lent(2, h)
        give_back(1, 2, h)

    own_partials(2)

    def sent(src, dst, src_slab, dst_slab, x, h):
        cross_all(src, dst, x, h).wait_send()
        both_sides(lambda side: slab_copy(src_slab, dst_slab, x, h, side).wait_send())

    for h in range(2):
        for e in range(LENDS):
            sent(lend_buf.at[e], land.at[e], lend_slab.at[e], land_slab.at[e], e, h)
        for a in range(BACKS):
            sent(back_buf.at[a], ret.at[a], back_slab.at[a], ret_slab.at[a], LENDS + a, h)


    @pl.loop(0, rows // 4)
    def _(g):
        for t in range(4):
            i = 4 * g + t
            acc[i] = ext1[i].astype(F32) + part[i].astype(F32)

    for h in range(2):
        both_sides(lambda side: slab_got(back_slab.at[1], ret_slab.at[1], LENDS + 1, h, side).wait_recv())
    for side in range(2):
        for u in range(opairs):
            two = apart(1, lambda hh: ret_slab[1, hh, side, u])
            for t in range(2):
                i = side * (rows - ovl) + 2 * u + t
                acc[i] = acc[i] + two[t].astype(F32)

    @pl.loop(1, n)
    def _(d):
        cross_got(back_buf.at[1], ret.at[1], LENDS + 1, 0, d).wait_recv()

    chain_returns(1, 1)

    @pl.loop(0, rows // 8)
    def _(g):
        for t in range(8):
            i = 8 * g + t
            out_ref[0, 0, i] = (acc[i] + run[last[i]]).astype(BF16)


def solution(mesh):
    n_slab = mesh.shape["slab"]
    n = mesh.shape["cross"]

    def per_device(rhs, m_blocks, m_cols, j_blocks, j_cols, send_list, send_count):
        rows, blk, nv = rhs.shape[2:]
        total_rows, kcount = m_blocks.shape[2:4]
        cap = send_list.shape[3]
        ovl = (total_rows - rows - n * cap) // 2
        slots = (n - 1) * cap
        tile = (blk, nv)
        smem = pl.BlockSpec(memory_space=pltpu.SMEM)
        hbm = pl.BlockSpec(memory_space=pltpu.HBM)
        return pl.pallas_call(
            functools.partial(kernel, n_slab, n, ovl, cap),
            out_shape=pltpu.VMEM(rhs.shape, rhs.dtype),
            in_specs=[hbm, hbm, hbm, smem, smem, smem, smem],
            out_specs=pl.BlockSpec(memory_space=pltpu.VMEM),
            scratch_shapes=[
                pltpu.VMEM(m_blocks.shape[2:], BF16),
                pltpu.VMEM(j_blocks.shape[2:], BF16),
                *([pltpu.VMEM((total_rows,) + tile, BF16)] * LENDS),
                pltpu.VMEM((rows,) + tile, BF16),
                pltpu.VMEM((rows,) + tile, F32),
                pltpu.VMEM((slots + 1,) + tile, F32),
                *([pltpu.VMEM((LENDS, 2, n - 1, cap // 2) + tile, BF16)] * 2),
                *([pltpu.VMEM((LENDS, 2, 2, ovl // 2) + tile, BF16)] * 2),
                *([pltpu.VMEM((BACKS, 2, n - 1, cap // 2) + tile, BF16)] * 2),
                *([pltpu.VMEM((BACKS, 2, 2, ovl // 2) + tile, BF16)] * 2),
                pltpu.SMEM((slots,), jnp.int32),
                pltpu.SMEM((rows,), jnp.int32),
                pltpu.SemaphoreType.DMA((3,)),
                pltpu.SemaphoreType.DMA((LENDS + BACKS, 2, n + 2)),
                pltpu.SemaphoreType.DMA((LENDS + BACKS, 2, n + 2)),
                pltpu.SemaphoreType.REGULAR,
                pltpu.SemaphoreType.REGULAR,
                pltpu.SemaphoreType.REGULAR,
            ],
            compiler_params=pltpu.CompilerParams(
                collective_id=0, has_side_effects=True, vmem_limit_bytes=60 * 1024 * 1024
            ),
        )(
            rhs, m_blocks, j_blocks, m_cols.transpose(0, 3, 1, 2), j_cols.transpose(0, 3, 1, 2),
            send_list.transpose(0, 1, 3, 2), send_count,
        )

    return jax.shard_map(
        per_device,
        mesh=mesh,
        in_specs=(
            P("slab", "cross", None, None, None),
            P("slab", "cross", None, None, None, None),
            P("slab", "cross", None, None),
            P("slab", "cross", None, None, None, None),
            P("slab", "cross", None, None),
            P("slab", "cross", None, None),
            P("slab", "cross", None),
        ),
        out_specs=P("slab", "cross", None, None, None),
        check_vma=False,
    )
```

```python
import functools

import jax
import jax.numpy as jnp
from jax import lax
from jax.experimental import pallas as pl
from jax.experimental.pallas import tpu as pltpu
from jax.sharding import PartitionSpec as P

MESH = pl.DeviceIdType.MESH
F32 = jnp.float32
BF16 = jnp.bfloat16

LENDS = 3
BACKS = 2


def kernel(
    n_slab, n, ovl, cap,
    rhs_hbm, m_hbm, j_hbm, m_cols, j_cols, targets, counts,
    acc, run, last,
    m_v, j_v, ext0, ext1, ext2, part,
    lend_buf, land, lend_slab, land_slab, back_buf, ret, back_slab, ret_slab,
    prev, load_sem, send_sem, recv_sem, ends_in, rest_in, down_in,
):
    s = lax.axis_index("slab")
    c = lax.axis_index("cross")
    ext = (ext0, ext1, ext2)
    rows = part.shape[0]
    blk, nv = part.shape[1:]
    half = nv // 2
    kcount = m_v.shape[1]
    pairs = cap // 2
    opairs = ovl // 2
    base = rows + 2 * ovl
    slots = (n - 1) * cap
    zero_slot = slots
    up_i, down_i = n, n + 1
    has_up = s > 0
    has_down = s < n_slab - 1

    assert n >= 4 and n & (n - 1) == 0
    centre = jnp.logical_and(c >= n // 4, c < n - n // 4)
    shift = jnp.where(centre, n // 2 - 1, 0)

    def peer(d):
        return jnp.bitwise_xor(c, d)

    def order(t, shift=shift):
        return lax.rem(t + shift, n - 1) + 1

    last_shift = jnp.where(centre, 2 * (n // 4) - 1, 3 * (n // 4) - 1)

    def grouped(do):
        do([0])
        pairs_of = (n - 2) // 2

        @pl.loop(0, pairs_of)
        def _(g):
            do([1 + 2 * g, 2 + 2 * g])

        for t in range(1 + 2 * pairs_of, n - 1):
            do([t])

    load_rhs = pltpu.make_async_copy(rhs_hbm.at[0, 0], ext0.at[pl.ds(0, rows)], load_sem.at[0])
    load_m = pltpu.make_async_copy(m_hbm.at[0, 0], m_v, load_sem.at[1])
    load_j = pltpu.make_async_copy(j_hbm.at[0, 0], j_v, load_sem.at[2])
    load_rhs.start()

    barrier = pltpu.get_barrier_semaphore()

    def greet(sem, to_slab, to_cross):
        pl.semaphore_signal(sem, inc=1, device_id=(to_slab, to_cross), device_id_type=MESH)

    quarter = n // 4
    centre_first = quarter
    centre_count = n // 2

    @pl.when(centre)
    def _():
        @pl.loop(1, n)
        def _(d):
            greet(barrier, s, lax.rem(c + d, n))

    @pl.when(has_down)
    def _():
        greet(barrier, s + 1, c)

    def pass_barrier():
        expected = centre_count - centre.astype(jnp.int32) + has_up.astype(jnp.int32)
        pl.semaphore_wait(barrier, expected)

        @pl.when(jnp.logical_not(centre))
        def _():
            @pl.loop(centre_first, centre_first + centre_count)
            def _(q):
                greet(ends_in, s, q)

        @pl.when(has_up)
        def _():
            greet(down_in, s - 1, c)

    def hear_ends():
        pl.semaphore_wait(ends_in, n - centre_count)
        greet(rest_in, s, jnp.where(c < n // 2, c - quarter, c + quarter))


    def swap(x):
        return pltpu.roll(x, half, 1)

    def low(dtype):
        return lax.broadcasted_iota(jnp.int32, (blk, nv), 1) < half

    def pack(h, r0, r1):
        if h == 0:
            return jnp.where(low(r0.dtype), r0, swap(r1))
        return jnp.where(low(r0.dtype), swap(r0), r1)

    def apart(h, tile_of):
        a = tile_of(0)
        if h == 0:
            return a, swap(a)
        b = tile_of(1)
        mask = low(a.dtype)
        return jnp.where(mask, a, swap(b)), jnp.where(mask, swap(a), b)


    def cross_copy(src, dst, x, h, d):
        return pltpu.make_async_remote_copy(
            src_ref=src.at[h, d - 1], dst_ref=dst.at[h, d - 1],
            send_sem=send_sem.at[x, h, 0], recv_sem=recv_sem.at[x, h, 0 if x < LENDS else d],
            device_id=(s, peer(d)), device_id_type=MESH,
        )

    def cross_all(src, dst, x, h):
        return pltpu.make_async_remote_copy(
            src_ref=src.at[h], dst_ref=dst.at[h],
            send_sem=send_sem.at[x, h, 0], recv_sem=recv_sem.at[x, h, 0],
            device_id=(s, peer(1)), device_id_type=MESH,
        )

    def cross_got(src, dst, x, h, d):
        return pltpu.make_async_remote_copy(
            src_ref=src.at[h, d - 1], dst_ref=dst.at[h, d - 1],
            send_sem=send_sem.at[x, h, 0], recv_sem=recv_sem.at[x, h, d],
            device_id=(s, peer(d)), device_id_type=MESH,
        )

    def slab_copy(src, dst, x, h, side):
        other = 1 - side
        return pltpu.make_async_remote_copy(
            src_ref=src.at[h, side], dst_ref=dst.at[h, other],
            send_sem=send_sem.at[x, h, n + side], recv_sem=recv_sem.at[x, h, n + other],
            device_id=(s - 1 + 2 * side, c), device_id_type=MESH,
        )

    def slab_got(src, dst, x, h, side):
        return pltpu.make_async_remote_copy(
            src_ref=src.at[h, side], dst_ref=dst.at[h, side],
            send_sem=send_sem.at[x, h, n + side], recv_sem=recv_sem.at[x, h, n + side],
            device_id=(s - 1 + 2 * side, c), device_id_type=MESH,
        )

    def both_sides(do):
        @pl.when(has_up)
        def _():
            do(0)

        @pl.when(has_down)
        def _():
            do(1)

    def pack_lent(e, h, d):
        q = peer(d)

        def picked(t):
            row = ext[e][targets[0, 0, t, q]]
            return jnp.where(t < counts[0, 0, q], row, jnp.zeros_like(row))

        for u in range(pairs):
            lend_buf[e, h, d - 1, u] = pack(h, picked(2 * u), picked(2 * u + 1))

    def pack_slab(e, h):
        for side in range(2):
            first_row = side * (rows - ovl)
            for u in range(opairs):
                r0 = first_row + 2 * u
                lend_slab[e, h, side, u] = pack(h, ext[e][r0], ext[e][r0 + 1])

    def send_slab(e, h):
        both_sides(lambda side: slab_copy(lend_slab.at[e], land_slab.at[e], e, h, side).start())

    def lend(e, h):
        def some(steps):
            ds = [order(t) for t in steps]
            for d in ds:
                pack_lent(e, h, d)
            for d in ds:
                cross_copy(lend_buf.at[e], land.at[e], e, h, d).start()

        grouped(some)
        pack_slab(e, h)
        send_slab(e, h)

    def await_lent(e, h):
        both_sides(lambda side: slab_got(lend_slab.at[e], land_slab.at[e], e, h, side).wait_recv())
        for side in range(2):
            for u in range(opairs):
                r0, r1 = apart(h, lambda hh: land_slab[e, hh, side, u])
                i = rows + side * ovl + 2 * u
                ext[e][i] = r0
                ext[e][i + 1] = r1
        cross_all(lend_buf.at[e], land.at[e], e, h).wait_recv()

        def some(steps):
            for t in steps:
                d = t + 1
                for u in range(pairs):
                    r0, r1 = apart(h, lambda hh: land[e, hh, d - 1, u])
                    i = base + peer(d) * cap + 2 * u
                    ext[e][i] = r0
                    ext[e][i + 1] = r1

        grouped(some)

    def row_product(blocks, cols, e, i, k0=0):
        left = jnp.concatenate([blocks[i, k] for k in range(k0, kcount)], axis=1)
        right = jnp.concatenate([ext[e][cols[0, k, 0, i]] for k in range(k0, kcount)], axis=0)
        return jnp.dot(left, right, preferred_element_type=F32)

    def packed_product(a, e, h, i):
        return pack(h, row_product(m_v, m_cols, e, i), row_product(m_v, m_cols, e, i + 1)).astype(BF16)

    def give_back(a, e, h):
        x = LENDS + a

        def some(steps):
            ds = [order(t, last_shift if a == 1 else shift) for t in steps]
            for d in ds:
                for u in range(pairs):
                    back_buf[a, h, d - 1, u] = packed_product(a, e, h, base + peer(d) * cap + 2 * u)
            for d in ds:
                cross_copy(back_buf.at[a], ret.at[a], x, h, d).start()

        grouped(some)

        @pl.loop(0, 2)
        def _(side):
            for u in range(opairs):
                back_slab[a, h, side, u] = packed_product(a, e, h, rows + side * ovl + 2 * u)

        both_sides(lambda side: slab_copy(back_slab.at[a], ret_slab.at[a], x, h, side).start())

    def own_partials(e):
        @pl.loop(0, rows // 8)
        def _(g):
            for t in range(8):
                i = 8 * g + t
                part[i] = row_product(m_v, m_cols, e, i).astype(BF16)

    def chain_returns(a, h):
        x = LENDS + a

        @pl.loop(1, n)
        def _(d):
            cross_got(back_buf.at[a], ret.at[a], x, h, d).wait_recv()
            for u in range(pairs):
                two = apart(h, lambda hh: ret[a, hh, d - 1, u])
                for t in range(2):
                    p = (d - 1) * cap + 2 * u + t
                    run[p] = two[t].astype(F32) + run[prev[p]]

    def await_returns(a, h):
        chain_returns(a, h)
        both_sides(lambda side: slab_got(back_slab.at[a], ret_slab.at[a], LENDS + a, h, side).wait_recv())

    def assembled(a, h, body):
        def total(i):
            return part[i].astype(F32) + run[last[i]]

        for side in range(2):
            for u in range(opairs):
                two = apart(h, lambda hh: ret_slab[a, hh, side, u])
                for t in range(2):
                    i = side * (rows - ovl) + 2 * u + t
                    body(i, total(i) + two[t].astype(F32))

        @pl.loop(0, (rows - 2 * ovl) // 4)
        def _(g):
            for t in range(4):
                i = ovl + 4 * g + t
                body(i, total(i))

    pass_barrier()
    load_rhs.wait()
    load_m.start()
    load_j.start()

    def lend_some(h, low_d, high_d):
        @pl.loop(low_d, high_d)
        def _(d):
            pack_lent(0, h, d)
            cross_copy(lend_buf.at[0], land.at[0], 0, h, d).start()


    @pl.when(centre)
    def _():
        lend_some(0, 3 * quarter, n)
        lend_some(1, 3 * quarter, n)
        hear_ends()
        for h in range(2):
            lend_some(h, 2 * quarter, 3 * quarter)
            lend_some(h, 1, 2 * quarter)

    @pl.when(jnp.logical_not(centre))
    def _():
        lend_some(0, quarter, 3 * quarter)
        pl.semaphore_wait(rest_in, 1)
        lend_some(0, 3 * quarter, n)
        lend_some(0, 1, quarter)
        lend_some(1, quarter, n)
        lend_some(1, 1, quarter)

    @pl.when(has_down)
    def _():
        pl.semaphore_wait(down_in, 1)

    for h in range(2):
        pack_slab(0, h)
        send_slab(0, h)

    zero_tile = jnp.zeros((blk, nv), BF16)
    for e in range(LENDS):
        for t in range(cap):
            ext[e][base + c * cap + t] = zero_tile

    def clear_slab(side):
        for h in range(2):
            for u in range(opairs):
                for e in range(LENDS):
                    land_slab[e, h, side, u] = zero_tile
                for a in range(BACKS):
                    ret_slab[a, h, side, u] = zero_tile

    @pl.when(jnp.logical_not(has_up))
    def _():
        clear_slab(0)

    @pl.when(jnp.logical_not(has_down))
    def _():
        clear_slab(1)

    run[zero_slot] = jnp.zeros((blk, nv), F32)

    def key_of(p):
        q = peer(p // cap + 1)
        t = lax.rem(p, cap)
        return jnp.where(t < counts[0, 0, q], targets[0, 0, t, q], -1)

    keys = [key_of(p) for p in range(slots)]
    for p in range(slots):
        found = zero_slot
        for p2 in range(p):
            found = jnp.where(keys[p2] == keys[p], p2, found)
        prev[p] = jnp.where(keys[p] < 0, zero_slot, found)

    @pl.loop(0, rows)
    def _(i):
        found = zero_slot
        for p in range(slots):
            found = jnp.where(keys[p] == i, p, found)
        last[i] = found

    load_m.wait()
    load_j.wait()

    await_lent(0, 0)
    give_back(0, 0, 0)
    await_lent(0, 1)
    give_back(0, 0, 1)
    own_partials(0)

    def put_first(i, value):
        ext1[i] = value.astype(BF16)

    for h in range(2):
        await_returns(0, h)
        assembled(0, h, put_first)
        lend(1, h)

    @pl.loop(0, rows // 16)
    def _(g):
        for t in range(16):
            i = 16 * g + t
            acc[i] = ext0[i].astype(F32) - jnp.dot(j_v[i, 0], ext1[i], preferred_element_type=F32)

    for h in range(2):
        await_lent(1, h)

        @pl.loop(0, rows // 16)
        def _(g):
            for t in range(16):
                i = 16 * g + t
                ext2[i] = (acc[i] - row_product(j_v, j_cols, 1, i, 1)).astype(BF16)

        lend(2, h)

    for h in range(2):
        await_lent(2, h)
        give_back(1, 2, h)

    own_partials(2)

    def sent(src, dst, src_slab, dst_slab, x, h):
        cross_all(src, dst, x, h).wait_send()
        both_sides(lambda side: slab_copy(src_slab, dst_slab, x, h, side).wait_send())

    for h in range(2):
        for e in range(LENDS):
            sent(lend_buf.at[e], land.at[e], lend_slab.at[e], land_slab.at[e], e, h)
        for a in range(BACKS):
            sent(back_buf.at[a], ret.at[a], back_slab.at[a], ret_slab.at[a], LENDS + a, h)


    @pl.loop(0, rows // 4)
    def _(g):
        for t in range(4):
            i = 4 * g + t
            acc[i] = ext1[i].astype(F32) + part[i].astype(F32)

    for h in range(2):
        both_sides(lambda side: slab_got(back_slab.at[1], ret_slab.at[1], LENDS + 1, h, side).wait_recv())
    for side in range(2):
        for u in range(opairs):
            two = apart(1, lambda hh: ret_slab[1, hh, side, u])
            for t in range(2):
                i = side * (rows - ovl) + 2 * u + t
                acc[i] = acc[i] + two[t].astype(F32)

    @pl.loop(1, n)
    def _(d):
        cross_got(back_buf.at[1], ret.at[1], LENDS + 1, 0, d).wait_recv()

    chain_returns(1, 1)


def finish(parts, acc, run, last, out_hbm, out_v, sems):
    share = out_v.shape[0] // parts

    def write(g):
        some = pl.ds(g * share, share)
        return pltpu.make_async_copy(out_v.at[some], out_hbm.at[0, 0, some], sems.at[g])

    for g in range(parts):
        for t in range(share):
            i = g * share + t
            out_v[i] = (acc[i] + run[last[i]]).astype(BF16)
        write(g).start()
    for g in range(parts):
        write(g).wait()


def solution(mesh):
    n_slab = mesh.shape["slab"]
    n = mesh.shape["cross"]

    def per_device(rhs, m_blocks, m_cols, j_blocks, j_cols, send_list, send_count):
        rows, blk, nv = rhs.shape[2:]
        total_rows, kcount = m_blocks.shape[2:4]
        cap = send_list.shape[3]
        ovl = (total_rows - rows - n * cap) // 2
        slots = (n - 1) * cap
        tile = (blk, nv)
        smem = pl.BlockSpec(memory_space=pltpu.SMEM)
        hbm = pl.BlockSpec(memory_space=pltpu.HBM)
        vmem = pl.BlockSpec(memory_space=pltpu.VMEM)
        sums = pl.pallas_call(
            functools.partial(kernel, n_slab, n, ovl, cap),
            out_shape=[
                pltpu.VMEM((rows,) + tile, F32),
                pltpu.VMEM((slots + 1,) + tile, F32),
                pltpu.SMEM((rows,), jnp.int32),
            ],
            in_specs=[hbm, hbm, hbm, smem, smem, smem, smem],
            out_specs=[vmem, vmem, smem],
            scratch_shapes=[
                pltpu.VMEM(m_blocks.shape[2:], BF16),
                pltpu.VMEM(j_blocks.shape[2:], BF16),
                *([pltpu.VMEM((total_rows,) + tile, BF16)] * LENDS),
                pltpu.VMEM((rows,) + tile, BF16),
                *([pltpu.VMEM((LENDS, 2, n - 1, cap // 2) + tile, BF16)] * 2),
                *([pltpu.VMEM((LENDS, 2, 2, ovl // 2) + tile, BF16)] * 2),
                *([pltpu.VMEM((BACKS, 2, n - 1, cap // 2) + tile, BF16)] * 2),
                *([pltpu.VMEM((BACKS, 2, 2, ovl // 2) + tile, BF16)] * 2),
                pltpu.SMEM((slots,), jnp.int32),
                pltpu.SemaphoreType.DMA((3,)),
                pltpu.SemaphoreType.DMA((LENDS + BACKS, 2, n + 2)),
                pltpu.SemaphoreType.DMA((LENDS + BACKS, 2, n + 2)),
                pltpu.SemaphoreType.REGULAR,
                pltpu.SemaphoreType.REGULAR,
                pltpu.SemaphoreType.REGULAR,
            ],
            compiler_params=pltpu.CompilerParams(
                collective_id=0, has_side_effects=True, vmem_limit_bytes=60 * 1024 * 1024
            ),
        )(
            rhs, m_blocks, j_blocks, m_cols.transpose(0, 3, 1, 2), j_cols.transpose(0, 3, 1, 2),
            send_list.transpose(0, 1, 3, 2), send_count,
        )
        parts = 4
        return pl.pallas_call(
            functools.partial(finish, parts),
            out_shape=jax.ShapeDtypeStruct(rhs.shape, rhs.dtype),
            in_specs=[vmem, vmem, smem],
            out_specs=hbm,
            scratch_shapes=[
                pltpu.VMEM((rows,) + tile, BF16),
                pltpu.SemaphoreType.DMA((parts,)),
            ],
            compiler_params=pltpu.CompilerParams(vmem_limit_bytes=16 * 1024 * 1024),
        )(*[pltpu.with_memory_space_constraint(v, pltpu.VMEM) for v in sums[:2]], sums[2])

    return jax.shard_map(
        per_device,
        mesh=mesh,
        in_specs=(
            P("slab", "cross", None, None, None),
            P("slab", "cross", None, None, None, None),
            P("slab", "cross", None, None),
            P("slab", "cross", None, None, None, None),
            P("slab", "cross", None, None),
            P("slab", "cross", None, None),
            P("slab", "cross", None),
        ),
        out_specs=P("slab", "cross", None, None, None),
        check_vma=False,
    )
```
